128 devices in a mesh: sec: 4 (over z), dev: 32 (over x, y, core).
Axes of the slice: x: 4, y: 4, z: 4, core: 2. Of those that a mesh axis runs over, the one named last changes fastest.
Arguments:
- x_input: bfloat16 [262144, 2048], P(('sec', 'dev'))
- log_decay: float32 [262144, 32], P(('sec', 'dev')), as said below
- b_input: bfloat16 [262144, 64], P(('sec', 'dev')), may hold values from -6 to 6
- c_input: bfloat16 [262144, 64], P(('sec', 'dev')), may hold values from -0.75 to 0.75
- skip_gain: float32 [32], replicated, may hold values from 0.5 to 2
- score_weight: bfloat16 [2048], replicated, may hold values from -0.125 to 0.125
- trace_lengths: int32 [4], replicated, may hold values from 1 to 131072, 262144 in all
- step_lengths: int32 [2048], replicated, may hold values from 1 to 512, 262144 in all
- step_slot: int32 [2048], replicated, may hold values from 0 to 2047, each once
Outputs:
- y_output: bfloat16 [262144, 2048], P(('sec', 'dev'))
- step_scores: float32 [2048], P(('sec', 'dev'))
The draws below stay inside these ranges and needn't reach their ends.
Inputs may be any that keep to these rules, and one draw needn't show every extreme that they name: `trace_lengths`: the lengths sum to 262144; one trace has exactly 131072 tokens. `step_lengths`: the lengths sum to 262144; some step has exactly 512 tokens. `step_slot`: each slot is named by exactly one step. `log_decay`: every entry is negative.
All inputs are finite; a program needn't handle non-finite values.
Results may differ from the reference program's by a relative error of at most 0.0053.
Values sent between devices are 32-bit elements; how exact they have to be, the bound alone decides.
No kernel may reach another device: no remote copies, remote signals or barrier semaphores. Data moves between devices by JAX's collectives and lax.ppermute only.
A program may use at most 384 MiB of HBM per device.

```python
import math
import jax
import jax.numpy as jnp
import numpy as np
from jax import lax

H = 32
P_SIZE = 64
N = 64
GROUP = 256
TRACES = 4
STEP_MOST = 512
TOK_DEV = 2048
TOKENS = 262144
STEPS = 2048


def head_rates(key):
    kind = jax.random.uniform(jax.random.fold_in(key, 11), (H,))
    share = 0.5
    top = 6.0
    slow = kind < share
    slow_rate = jnp.exp(jax.random.uniform(jax.random.fold_in(key, 12), (H,), minval=math.log(0.25), maxval=math.log(top))) / TOKENS
    fast_rate = 1.0 / jnp.exp(jax.random.uniform(jax.random.fold_in(key, 13), (H,), minval=math.log(30.0), maxval=math.log(50.0)))
    return jnp.where(slow, slow_rate, fast_rate)


def draw_log_decay(key, part):
    attenuation_speeds = head_rates(key)
    position_attenuation_multiplier = jnp.exp(jax.random.uniform(jax.random.fold_in(key, 21), (TOKENS, H), minval=math.log(0.5), maxval=math.log(2.0)))
    blocks = TOKENS // TOK_DEV
    tile_attenuation_multiplier = jnp.exp(jax.random.uniform(jax.random.fold_in(key, 22), (blocks, H), minval=math.log(0.5), maxval=math.log(2.0)))
    tile_attenuation_multiplier = jnp.repeat(tile_attenuation_multiplier, TOK_DEV, axis=0)
    places = jax.random.randint(jax.random.fold_in(key, 23), (4,), 0, TOKENS)
    piece_extents = jnp.exp(jax.random.uniform(jax.random.fold_in(key, 24), (4,), minval=math.log(0.22), maxval=math.log(0.7)))
    equality_indicator = jnp.arange(TOKENS, dtype=jnp.int32)[:, None] == places[None, :]
    contiguous_span_piece = jnp.sum(jnp.where(equality_indicator, piece_extents[None, :], 0.0), axis=1)
    payload_vectors = -(attenuation_speeds[None, :] * position_attenuation_multiplier * tile_attenuation_multiplier) - contiguous_span_piece[:, None]
    return payload_vectors.astype(jnp.float32)


def draw_x_input(key, part):
    attenuation_speeds = head_rates(key)
    sigma = jnp.sqrt(2.0 * jnp.maximum(attenuation_speeds, 2.0 / TOKENS))
    noise = jax.random.normal(jax.random.fold_in(key, 31), (TOKENS, H, P_SIZE))
    payload_vectors = noise * sigma[None, :, None]
    return payload_vectors.reshape(TOKENS, H * P_SIZE).astype(jnp.bfloat16)


def block_scale(key, extent, split, least, largest):
    loudness, own = 1.0, jax.random.fold_in(key, 6)
    for dim, shards_of in split:
        steps = jnp.exp(jax.random.uniform(jax.random.fold_in(own, dim), (shards_of,), jnp.float32, least / len(split), largest / len(split)))
        loudness = loudness * jnp.repeat(steps, extent[dim] // shards_of).reshape([-1 if axis == dim else 1 for axis in range(len(extent))])
    return loudness


def split_up(count, total, limit, skew):
    weights = [(1 << 20) // math.isqrt(standing ** skew) + 1 for standing in range(2, count + 1)]
    spare, holding = total - limit - (count - 1), [1] * (count - 1)
    while spare > 0:
        movable = [i for i in range(count - 1) if holding[i] < limit]
        whole, budget = sum([weights[i] for i in movable]), spare
        for i in movable:
            extra = min(limit - holding[i], max(1, budget * weights[i] // whole), spare)
            holding[i] = holding[i] + extra
            spare = spare - extra
    return np.array([limit] + holding)


def ragged_sizes(key, count, total, bound, slope):
    if count == 2:
        one = jax.random.randint(key, (), max(1, total - bound), min(bound, total - 1) + 1)
        return jnp.stack([one, total - one])
    sizes = jnp.asarray(split_up(count, total, bound, slope), jnp.int32)
    pairs = (count - 1) // 2
    donor, sink = sizes[1:1 + 2 * pairs:2], sizes[2:2 + 2 * pairs:2]
    room = jnp.minimum(donor - 1, bound - sink)
    moved = jax.random.randint(jax.random.fold_in(key, 1), (pairs,), 0, 1 << 20) % (room + 1)
    sizes = sizes.at[1:1 + 2 * pairs:2].set(donor - moved).at[2:2 + 2 * pairs:2].set(sink + moved)
    return sizes[jax.random.permutation(jax.random.fold_in(key, 2), count)]


def bell_draw(own_key, shape, deviation, most, split=(), kind=jnp.bfloat16):
    result = deviation * jax.random.normal(own_key, shape, jnp.float32)
    if split:
        result = result * block_scale(own_key, shape, split, -0.22, 0.18)
    return jnp.clip(result, -most, most).astype(kind)


def setup_inputs(seed: int = 0) -> dict:
    seeds = jax.random.split(jax.random.key(seed), 10)
    x_input = draw_x_input(jax.random.fold_in(seeds[9], 71), 0)
    log_decay = draw_log_decay(jax.random.fold_in(seeds[9], 71), 0)
    b_input = bell_draw(seeds[2], (TOKENS, N), 1.0, 6.0, ((0, 128),))
    c_input = bell_draw(seeds[3], (TOKENS, N), N ** -0.5, 0.75, ((0, 128),))
    skip_gain = jnp.clip(jax.random.uniform(seeds[4], (H,), jnp.float32, 0.5, 2.0), 0.5, 2.0)
    score_weight = bell_draw(seeds[5], (H * P_SIZE,), (H * P_SIZE) ** -0.5, 0.125)
    trace_lengths = ragged_sizes(seeds[6], TRACES, TOKENS, TOKENS // 2, 1).astype(jnp.int32)
    step_lengths = ragged_sizes(seeds[7], STEPS, TOKENS, STEP_MOST, 2).astype(jnp.int32)
    step_slot = jax.random.permutation(seeds[8], STEPS).astype(jnp.int32)
    return {"x_input": x_input, "log_decay": log_decay, "b_input": b_input, "c_input": c_input, "skip_gain": skip_gain, "score_weight": score_weight, "trace_lengths": trace_lengths, "step_lengths": step_lengths, "step_slot": step_slot}


def trace_ids(starts, positions):
    return jnp.sum((starts[None, :] <= positions[:, None]).astype(jnp.int32), axis=1)


def group_terms(x_group, decay_group, b_group, c_group, trace_group, prev_trace):
    length = x_group.shape[0]
    cum = jnp.cumsum(decay_group, axis=0)
    cum_heads = cum.T
    order = jnp.arange(length, dtype=jnp.int32)
    keep = (order[:, None] >= order[None, :]) & (trace_group[:, None] == trace_group[None, :])
    gram = jnp.dot(c_group, b_group.T, preferred_element_type=jnp.float32)
    diff = cum_heads[:, :, None] - cum_heads[:, None, :]
    decay = jnp.exp(jnp.where(keep[None], diff, -jnp.inf))
    weight = lax.optimization_barrier((gram[None] * decay).astype(jnp.bfloat16))
    x_heads = x_group.reshape(length, H, P_SIZE)
    intra = jnp.einsum("hts,shp->thp", weight.astype(jnp.float32), x_heads.astype(jnp.float32))
    to_end = jnp.exp(cum[-1][None, :] - cum) * (trace_group == trace_group[-1]).astype(jnp.float32)[:, None]
    scaled = lax.optimization_barrier((x_heads.astype(jnp.float32) * to_end[:, :, None]).astype(jnp.bfloat16))
    new_state = jnp.einsum("shp,sn->hpn", scaled.astype(jnp.float32), b_group.astype(jnp.float32))
    carry = jnp.exp(cum) * (trace_group == prev_trace).astype(jnp.float32)[:, None]
    return intra, new_state, carry


def reference(x_input, log_decay, b_input, c_input, skip_gain, score_weight, trace_lengths, step_lengths, step_slot):
    count = TOKENS // GROUP
    positions = jnp.arange(TOKENS, dtype=jnp.int32)
    starts = (jnp.cumsum(trace_lengths) - trace_lengths).astype(jnp.int32)
    trace = trace_ids(starts, positions).reshape(count, GROUP)
    prev = trace_ids(starts, (jnp.arange(count, dtype=jnp.int32) * GROUP - 1).astype(jnp.int32))
    inputs = (x_input.reshape(count, GROUP, H * P_SIZE), log_decay.reshape(count, GROUP, H),
              b_input.reshape(count, GROUP, N), c_input.reshape(count, GROUP, N), trace, prev)

    def advance(state, item):
        x_group, decay_group, b_group, c_group, trace_group, prev_trace = item
        intra, new_state, carry = group_terms(x_group, decay_group, b_group, c_group, trace_group, prev_trace)
        read_state = lax.optimization_barrier(state.astype(jnp.bfloat16))
        inter = jnp.einsum("tn,hpn->thp", c_group.astype(jnp.float32), read_state.astype(jnp.float32)) * carry[:, :, None]
        x_heads = x_group.reshape(GROUP, H, P_SIZE).astype(jnp.float32)
        y_group = (intra + inter + skip_gain[None, :, None] * x_heads).astype(jnp.bfloat16).reshape(GROUP, H * P_SIZE)
        following = carry[-1][:, None, None] * state + new_state
        return following, y_group

    first = jnp.zeros((H, P_SIZE, N), jnp.float32)
    last, y_blocks = lax.scan(advance, first, inputs)
    y_output = y_blocks.reshape(TOKENS, H * P_SIZE)
    score = jnp.dot(y_output, score_weight, preferred_element_type=jnp.float32)
    step_starts = (jnp.cumsum(step_lengths) - step_lengths).astype(jnp.int32)
    step_id = (jnp.searchsorted(step_starts, positions, side="right") - 1).astype(jnp.int32)
    totals = jax.ops.segment_sum(score, step_id, num_segments=STEPS)
    pooled = totals / step_lengths.astype(jnp.float32)
    step_scores = jnp.zeros((STEPS,), jnp.float32).at[step_slot].set(pooled)
    return y_output, step_scores
```

```python
import functools

import jax
import jax.numpy as jnp
from jax import lax
from jax.experimental import pallas as pl
from jax.experimental.pallas import tpu as pltpu
from jax.sharding import Mesh
from jax.sharding import PartitionSpec as P

SEC_DEV = ("sec", "dev_0", "dev_1", "dev_2")
CHUNK = 64
BLOCK = 256
LANES = 128
LOG2E = 1.4426950408889634
F32 = jnp.float32
BF16 = jnp.bfloat16


def iota(shape, dim):
    return lax.broadcasted_iota(jnp.int32, shape, dim)


def mm(a, b):
    return jnp.dot(a, b, preferred_element_type=F32)


def mm_nt(a, b):
    return lax.dot_general(a, b, (((1,), (1,)), ((), ())), preferred_element_type=F32)


def split(value, pieces):
    parts = []
    for _ in range(pieces - 1):
        part = value.astype(BF16)
        parts.append(part)
        value = value - part.astype(F32)
    parts.append(value.astype(BF16))
    return parts


def trace_of(starts, position):
    total = jnp.zeros_like(position)
    for start in starts:
        total = total + jnp.where(position >= start, 1, 0)
    return total


def expander(heads, head_size, copies):
    shape = (heads * copies, heads * head_size)
    same = (iota(shape, 0) % heads) == (iota(shape, 1) // head_size)
    return jnp.where(same, 1.0, 0.0).astype(BF16)


def local_kernel(
    lengths_ref, base_ref, x_ref, decay_ref, b_ref, c_ref, skip_ref,
    y_ref, reach_ref, message_ref,
    expand_ref, cum_ref, state_ref, total_ref, skip_row_ref,
):
    step = pl.program_id(0)
    heads = decay_ref.shape[1]
    width = x_ref.shape[1]
    head_size = width // heads
    n = b_ref.shape[1]
    base = base_ref[0]
    starts = []
    first = jnp.int32(0)
    for k in range(lengths_ref.shape[0]):
        starts.append(first)
        first = first + lengths_ref[k]

    @pl.when(step == 0)
    def _():
        expand_ref[...] = expander(heads, head_size, 3)
        state_ref[...] = jnp.zeros_like(state_ref)
        total_ref[...] = jnp.zeros_like(total_ref)
        gain = jnp.concatenate(split(jnp.broadcast_to(skip_ref[...], (8, heads)), 3), axis=1)
        skip_row_ref[...] = mm(gain, expand_ref[...])

    at_block = base + step * BLOCK
    logs = split(decay_ref[...] * LOG2E, 3)
    shape = (BLOCK, BLOCK)
    lower = iota(shape, 0) >= iota(shape, 1)
    same_chunk = (iota(shape, 0) // CHUNK) == (iota(shape, 1) // CHUNK)
    ones_all = jnp.where(lower, 1.0, 0.0).astype(BF16)
    ones_chunk = jnp.where(lower & same_chunk, 1.0, 0.0).astype(BF16)
    cum = mm(ones_chunk, logs[0]) + mm(ones_chunk, logs[1]) + mm(ones_chunk, logs[2])
    far = mm(ones_all, logs[0]) + mm(ones_all, logs[1]) + mm(ones_all, logs[2])
    far = far + total_ref[0:1, :]
    total_ref[...] = jnp.broadcast_to(far[BLOCK - 1 :, :], total_ref.shape)
    before = trace_of(starts, base - 1)
    block_pos = at_block + iota((BLOCK, heads), 0)
    reach = jnp.where(trace_of(starts, block_pos) == before, jnp.exp2(far), 0.0)
    reach_ref[...] = jnp.concatenate(split(reach, 2), axis=1)
    cum_ref[...] = mm(jnp.concatenate(split(cum, 3), axis=1), expand_ref[...])

    small = (CHUNK, LANES)
    row_id = iota(small, 0)
    col_id = iota(small, 1) % CHUNK
    causal = row_id >= col_id
    diagonal = row_id == col_id
    left = jnp.where(iota(small, 1) < CHUNK, 1.0, 0.0).astype(BF16)
    right = jnp.where(iota(small, 1) >= CHUNK, 1.0, 0.0).astype(BF16)

    def chunk(k, carry):
        row = pl.multiple_of(k * CHUNK, CHUNK)
        rows = pl.ds(row, CHUNK)
        pos = at_block + row
        tr_prev = trace_of(starts, pos - 1)
        tr_end = trace_of(starts, pos + CHUNK - 1)
        keep = causal & (trace_of(starts, pos + row_id) == trace_of(starts, pos + col_id))
        token = trace_of(starts, pos + iota((CHUNK, n), 0))
        c_chunk = c_ref[rows, :]
        b_chunk = b_ref[rows, :]
        gram = mm_nt(c_chunk, jnp.concatenate([b_chunk, b_chunk], axis=0))
        gram = jnp.where(keep, gram, 0.0)
        c_mask = jnp.where(token == tr_prev, c_chunk.astype(F32), 0.0).astype(BF16)
        b_mask = jnp.where(token == tr_end, b_chunk.astype(F32), 0.0).T.astype(BF16)
        goes_on = jnp.where(tr_end == tr_prev, 1.0, 0.0)
        for pair in range(width // LANES):
            lanes = slice(pair * LANES, (pair + 1) * LANES)
            ce = cum_ref[rows, lanes]
            end = ce[CHUNK - 1 :, :]
            across = jnp.sum(jnp.where(diagonal, ce, 0.0), axis=0, keepdims=True)
            from_start = jnp.exp2(ce)
            to_end = jnp.exp2(end - ce)
            x_pair = x_ref[rows, lanes]
            x_wide = x_pair.astype(F32)
            weight = (gram * jnp.exp2(jnp.minimum(ce - across, 0.0))).astype(BF16)
            x_diag = jnp.concatenate([x_pair * left, x_pair * right], axis=0)
            intra = mm(weight, x_diag)
            held = state_ref[:, lanes]
            inter = mm(c_mask, held.astype(BF16))
            y = intra + from_start * inter + skip_row_ref[0:1, lanes] * x_wide
            y_ref[rows, lanes] = y.astype(BF16)
            scaled = (x_wide * to_end).astype(BF16)
            factor = from_start[CHUNK - 1 :, :] * goes_on
            state_ref[:, lanes] = held * factor + mm(b_mask, scaled)
        return carry

    lax.fori_loop(0, BLOCK // CHUNK, chunk, 0)

    @pl.when(step == pl.num_programs(0) - 1)
    def _():
        last = reach[BLOCK - 8 :, :]
        whole = mm(jnp.concatenate(split(last, 3), axis=1), expand_ref[...])
        pairs = width // LANES
        for i in range(n // 8):
            for j in range(pairs):
                lanes = slice(j * LANES, (j + 1) * LANES)
                tile = state_ref[8 * i : 8 * i + 8, lanes]
                for k in range(8):
                    message_ref[i * pairs + j, :, k * LANES : (k + 1) * LANES] = tile[k : k + 1, :]
                message_ref[i * pairs + j, :, 8 * LANES :] = whole[7:8, lanes]


def prefix_kernel(got_ref, out_ref):
    def one(d, held):
        got = got_ref[d]
        factor = got[:, 8 * LANES :]
        following = []
        for k in range(8):
            lanes = slice(k * LANES, (k + 1) * LANES)
            out_ref[d, :, lanes] = held[k]
            following.append(held[k] * factor + got[:, lanes])
        return tuple(following)

    zero = jnp.zeros((1, LANES), F32)
    lax.fori_loop(0, got_ref.shape[0], one, (zero,) * 8, unroll=4)


def final_kernel(
    base_ref, y_in_ref, c_ref, reach_ref, back_ref, weight_ref, start_ref, length_ref, slot_ref,
    y_ref, spread_ref,
    expand_ref, gather_ref, state_ref, score_ref, weight_row_ref,
):
    step = pl.program_id(0)
    heads = reach_ref.shape[1] // 2
    width = y_ref.shape[1]
    n = c_ref.shape[1]
    pairs = width // LANES
    tokens = BLOCK * pl.num_programs(0)

    @pl.when(step == 0)
    def _():
        expand_ref[...] = expander(heads, width // heads, 2)
        weight_row_ref[...] = jnp.broadcast_to(
            weight_ref[...].astype(F32), weight_row_ref.shape
        )
        for i in range(n // 8):
            for j in range(pairs):
                piece = back_ref[i * pairs + j]
                for k in range(8):
                    gather_ref[8 * i + k : 8 * i + k + 1, j * LANES : (j + 1) * LANES] = piece[
                        :, k * LANES : (k + 1) * LANES
                    ]
        state_ref[...] = gather_ref[...].astype(BF16)

    c_block = c_ref[...]
    reach = reach_ref[...]
    total = jnp.zeros((BLOCK, LANES), F32)
    wide = 2 * LANES
    for part in range(width // wide):
        lanes = slice(part * wide, (part + 1) * wide)
        inter = mm(c_block, state_ref[:, lanes])
        gain = mm(reach, expand_ref[:, lanes])
        y = y_in_ref[:, lanes].astype(F32) + gain * inter
        y_ref[:, lanes] = y.astype(BF16)
        scored = y * weight_row_ref[0:1, lanes]
        total = total + scored[:, :LANES] + scored[:, LANES:]
    for k in range(BLOCK // LANES):
        turned = total[k * LANES : (k + 1) * LANES, :].T
        score_ref[pl.ds(step * (BLOCK // LANES) + k, 1), :] = jnp.sum(turned, axis=0, keepdims=True)

    @pl.when(step == pl.num_programs(0) - 1)
    def _():
        base = base_ref[0]
        steps = slot_ref.shape[1]
        slot_rows = steps // LANES
        slot = slot_ref[...]
        at = start_ref[...]
        span = length_ref[...]
        in_row = jnp.where(
            iota((slot_rows, steps), 0) == (slot >> 7), 1.0, 0.0
        )
        in_lane = jnp.where(iota((LANES, steps), 0) == (slot & 127), 1.0, 0.0).astype(BF16)
        found = []
        for value in (at >> 16, (at >> 8) & 255, at & 255, span >> 8, span & 255):
            found.append(mm_nt((in_row * value.astype(F32)).astype(BF16), in_lane))
        start = (found[0] * 65536.0 + found[1] * 256.0 + found[2]).astype(jnp.int32)
        length_f = found[3] * 256.0 + found[4]
        length = length_f.astype(jnp.int32)
        from_tok = jnp.clip(start - base, 0, tokens)
        to_tok = jnp.clip(start + length - base, 0, tokens)

        held = score_ref.shape[0]
        grown = held + 8
        score = score_ref[...]
        strict = jnp.where(iota((LANES, LANES), 0) < iota((LANES, LANES), 1), 1.0, 0.0)
        strict = strict.astype(BF16)
        ahead = jnp.where(iota((grown, held), 1) < iota((grown, held), 0), 1.0, 0.0).astype(BF16)
        inside = jnp.zeros((held, LANES), F32)
        offset = jnp.zeros((grown, LANES), F32)
        for piece in split(score, 3):
            inside = inside + mm(piece, strict)
            offset = offset + mm(ahead, piece)
        running = jnp.sum(offset, axis=1, keepdims=True) + jnp.concatenate(
            [inside, jnp.zeros((8, LANES), F32)], axis=0
        )
        table = split(running, 3)

        def look_up(index):
            pick = jnp.where(iota((LANES, LANES), 0) == (index & 127), 1.0, 0.0).astype(BF16)
            rows = mm(table[0], pick) + mm(table[1], pick) + mm(table[2], pick)
            mine = iota((grown, LANES), 0) == (index >> 7)
            return jnp.sum(jnp.where(mine, rows, 0.0), axis=0, keepdims=True)

        for r in range(slot_rows):
            value = look_up(to_tok[r : r + 1, :]) - look_up(from_tok[r : r + 1, :])
            spread_ref[r : r + 1, :] = value / length_f[r : r + 1, :]


def shards(
    x_input,
    log_decay,
    b_input,
    c_input,
    skip_gain,
    score_weight,
    trace_lengths,
    step_lengths,
    step_slot,
):
    rows, width = x_input.shape
    heads = log_decay.shape[1]
    n = b_input.shape[1]
    devices = lax.axis_size(SEC_DEV)
    index = lax.axis_index(SEC_DEV)
    base = (index * rows).astype(jnp.int32).reshape(1)
    blocks = rows // BLOCK
    tiles = (n // 8) * (width // LANES)
    smem = pl.BlockSpec(memory_space=pltpu.SMEM)

    def by_block(columns):
        return pl.BlockSpec((BLOCK, columns), lambda i: (i, 0))

    def whole(*shape):
        return pl.BlockSpec(shape, lambda i: (0,) * len(shape))

    params = pltpu.CompilerParams(
        dimension_semantics=("arbitrary",), vmem_limit_bytes=40 * 1024 * 1024
    )
    y_local, reach, message = pl.pallas_call(
        local_kernel,
        grid=(blocks,),
        in_specs=[
            smem, smem, by_block(width), by_block(heads), by_block(n), by_block(n), whole(1, heads),
        ],
        out_specs=[by_block(width), by_block(2 * heads), whole(tiles, 1, 9 * LANES)],
        out_shape=[
            jax.ShapeDtypeStruct((rows, width), BF16),
            jax.ShapeDtypeStruct((rows, 2 * heads), BF16),
            jax.ShapeDtypeStruct((tiles, 1, 9 * LANES), F32),
        ],
        scratch_shapes=[
            pltpu.VMEM((3 * heads, width), BF16),
            pltpu.VMEM((BLOCK, width), F32),
            pltpu.VMEM((n, width), F32),
            pltpu.VMEM((8, heads), F32),
            pltpu.VMEM((8, width), F32),
        ],
        compiler_params=params,
        name="local",
    )(trace_lengths, base, x_input, log_decay, b_input, c_input, skip_gain.reshape(1, heads))
    arrived = lax.all_to_all(message, SEC_DEV, split_axis=0, concat_axis=0, tiled=True)
    incoming = pl.pallas_call(
        prefix_kernel,
        out_shape=jax.ShapeDtypeStruct((devices, 1, 8 * LANES), F32),
        in_specs=[pl.BlockSpec(memory_space=pltpu.VMEM)],
        out_specs=pl.BlockSpec(memory_space=pltpu.VMEM),
        compiler_params=pltpu.CompilerParams(vmem_limit_bytes=8 * 1024 * 1024),
        name="prefix",
    )(arrived)
    back = lax.all_to_all(incoming, SEC_DEV, split_axis=0, concat_axis=0, tiled=True)
    steps = step_slot.shape[0]
    step_starts = (jnp.cumsum(step_lengths) - step_lengths).astype(jnp.int32)
    y_output, spread = pl.pallas_call(
        final_kernel,
        grid=(blocks,),
        in_specs=[
            smem, by_block(width), by_block(n), by_block(2 * heads),
            whole(tiles, 1, 8 * LANES), whole(1, width), whole(1, steps), whole(1, steps),
            whole(1, steps),
        ],
        out_specs=[by_block(width), whole(steps // LANES, LANES)],
        out_shape=[
            jax.ShapeDtypeStruct((rows, width), BF16),
            jax.ShapeDtypeStruct((steps // LANES, LANES), F32),
        ],
        scratch_shapes=[
            pltpu.VMEM((2 * heads, width), BF16),
            pltpu.VMEM((n, width), F32),
            pltpu.VMEM((n, width), BF16),
            pltpu.VMEM((rows // LANES, LANES), F32),
            pltpu.VMEM((8, width), F32),
        ],
        compiler_params=params,
        name="final",
    )(
        base, y_local, c_input, reach, back, score_weight.reshape(1, width),
        step_starts.reshape(1, steps), step_lengths.reshape(1, steps), step_slot.reshape(1, steps),
    )
    owned = steps // devices
    received = lax.all_to_all(
        spread.reshape(devices, 1, owned), SEC_DEV, split_axis=0, concat_axis=0, tiled=True
    )
    return (y_output, jnp.sum(received, axis=(0, 1)))


def solution(mesh):
    torus = Mesh(
        mesh.devices.reshape(mesh.shape["sec"], 4, 4, 2), ("sec", "dev_0", "dev_1", "dev_2")
    )
    in_specs = (P(SEC_DEV, None),) * 4 + (P(),) * 5
    out_specs = (P(SEC_DEV, None), P(SEC_DEV))
    return jax.shard_map(
        shards, mesh=torus, in_specs=in_specs, out_specs=out_specs, check_vma=False
    )
```
